32 devices in a mesh: dp: 16 (over z, y, x), fsdp: 2 (over core).
Axes of the slice: x: 2, y: 2, z: 4, core: 2. Of those that a mesh axis runs over, the one named last changes fastest.
Arguments:
- tokens: bfloat16 [64, 512, 768], P(('dp', 'fsdp')), may hold values from -6 to 6
- cotangent: bfloat16 [64, 80, 768], P(('dp', 'fsdp')), may hold values from -6 to 6
- positions: int32 [64, 80], P(('dp', 'fsdp')), may hold values from 0 to 511, as said below
- counts: int32 [64], P(('dp', 'fsdp')), may hold values from 40 to 80
- query_key_value_weight: bfloat16 [2, 768, 2304], P(None, ('dp', 'fsdp')), may hold values from -0.21875 to 0.21875
- attention_output_weight: bfloat16 [2, 768, 768], P(None, ('dp', 'fsdp')), may hold values from -0.625 to 0.625
- feedforward_input_weight: bfloat16 [2, 768, 3072], P(None, ('dp', 'fsdp')), may hold values from -0.21875 to 0.21875
- feedforward_input_bias: bfloat16 [2, 3072], P(None, ('dp', 'fsdp')), may hold values from -3 to 3
- feedforward_output_weight: bfloat16 [2, 3072, 768], P(None, ('dp', 'fsdp')), may hold values from -0.109375 to 0.109375
- small: bfloat16 [2, 768, 24], P(None, ('dp', 'fsdp'))
- query_up_weight: float32 [2, 8, 768], replicated, may hold values from -1.2 to 1.2
- value_up_weight: float32 [2, 8, 768], replicated, may hold values from -1.2 to 1.2
Outputs:
- activations: bfloat16 [64, 512, 768], P(('dp', 'fsdp'))
- d_tokens: float32 [64, 512, 768], P(('dp', 'fsdp'))
- query_up_gradient: float32 [2, 8, 768], replicated
- value_up_gradient: float32 [2, 8, 768], replicated
The draws below stay inside these ranges and needn't reach their ends.
Inputs may be any that keep to these rules, and one draw needn't show every extreme that they name: In each sequence the 80 entries are distinct positions; entry m is used where m < counts of that sequence.
All inputs are finite; a program needn't handle non-finite values.
Results may differ from the reference program's by a relative error of at most 0.03.
Values may be sent and summed in bfloat16 or wider, within the bound.
No kernel may reach another device: no remote copies, remote signals or barrier semaphores. Data moves between devices by JAX's collectives and lax.ppermute only.
A program may use at most 256 MiB of HBM per device.

```python
import math
import jax
import jax.numpy as jnp
from jax import lax

MODEL_WIDTH = 768
H = 12
HD = 64
FF = 3072
ADAPTER_RANK = 8
ENCODER_LAYERS = 2
LEN = 512
MAXM = 80
SEQS = 64


def draw_small(key, part):
    base = jax.random.normal(key, (ENCODER_LAYERS, MODEL_WIDTH, 8 + 2 * ADAPTER_RANK), jnp.float32)
    column = jnp.arange(8 + 2 * ADAPTER_RANK)
    is_gain = (column == 3) | (column == 6)
    is_down = column >= 8
    factor = jnp.where(is_down, MODEL_WIDTH ** (-0.5), jnp.where(is_gain, 0.1, 0.4))
    offset = jnp.where(is_gain, 1.0, 0.0)
    return (base * factor + offset).astype(jnp.bfloat16)


def draw_positions(key, part):
    scores = jax.random.randint(key, (SEQS, LEN), 0, 1 << 20) * LEN + jnp.arange(LEN, dtype=jnp.int32)[None, :]
    order = jnp.argsort(scores, axis=1)
    return order[:, :MAXM].astype(jnp.int32)


def draw_counts(key, part):
    first_key, second_key = jax.random.split(key)
    drawn = jax.random.randint(first_key, (SEQS,), MAXM // 2, MAXM + 1)
    chosen = jax.random.randint(second_key, (), 0, SEQS)
    places = jnp.arange(SEQS)
    drawn = jnp.where(places == chosen, MAXM, drawn)
    drawn = jnp.where(places == (chosen + 1) % SEQS, MAXM // 2, drawn)
    return drawn.astype(jnp.int32)


def block_scale(stream_key, extent, cuts, smallest, high):
    def one(position, shards_of):
        draws = jax.random.uniform(jax.random.fold_in(jax.random.fold_in(stream_key, 6), position), (shards_of,), jnp.float32, smallest / len(cuts), high / len(cuts))
        return jnp.repeat(jnp.exp(draws), extent[position] // shards_of).reshape((-1,) + (1,) * (len(extent) - position - 1))

    gain = one(*cuts[0])
    for cut in cuts[1:]:
        gain = gain * one(*cut)
    return gain


def normal_values(stream_key, dims, scale, most, pieces=(), kind=jnp.bfloat16):
    values = jax.random.normal(stream_key, dims, jnp.float32) * scale
    if len(pieces) > 0:
        values = block_scale(stream_key, dims, pieces, -0.22, 0.18) * values
    return jnp.clip(values, min=-most, max=most).astype(kind)


def setup_inputs(seed: int = 0) -> dict:
    splits = jax.random.split(jax.random.key(seed), 13)
    tokens = normal_values(splits[0], (SEQS, LEN, MODEL_WIDTH), 1.0, 6.0, ((0, 32),))
    cotangent = normal_values(splits[1], (SEQS, MAXM, MODEL_WIDTH), 1.0, 6.0, ((0, 32),))
    positions = draw_positions(jax.random.fold_in(splits[12], 71), 0)
    counts = draw_counts(jax.random.fold_in(splits[12], 71), 0)
    query_key_value_weight = normal_values(splits[4], (ENCODER_LAYERS, MODEL_WIDTH, 3 * MODEL_WIDTH), MODEL_WIDTH ** -0.5, 0.21875, ((1, 32),))
    attention_output_weight = normal_values(splits[5], (ENCODER_LAYERS, MODEL_WIDTH, MODEL_WIDTH), (MODEL_WIDTH // 8) ** -0.5, 0.625, ((1, 32),))
    feedforward_input_weight = normal_values(splits[6], (ENCODER_LAYERS, MODEL_WIDTH, FF), MODEL_WIDTH ** -0.5, 0.21875, ((1, 32),))
    feedforward_input_bias = normal_values(splits[7], (ENCODER_LAYERS, FF), 0.5, 3.0, ((1, 32),))
    feedforward_output_weight = normal_values(splits[8], (ENCODER_LAYERS, FF, MODEL_WIDTH), FF ** -0.5, 0.109375, ((1, 32),))
    small = draw_small(jax.random.fold_in(splits[12], 71), 0)
    query_up_weight = normal_values(splits[10], (ENCODER_LAYERS, ADAPTER_RANK, MODEL_WIDTH), 0.2, 1.2, (), jnp.float32)
    value_up_weight = normal_values(splits[11], (ENCODER_LAYERS, ADAPTER_RANK, MODEL_WIDTH), 0.2, 1.2, (), jnp.float32)
    return {"tokens": tokens, "cotangent": cotangent, "positions": positions, "counts": counts, "query_key_value_weight": query_key_value_weight, "attention_output_weight": attention_output_weight, "feedforward_input_weight": feedforward_input_weight, "feedforward_input_bias": feedforward_input_bias, "feedforward_output_weight": feedforward_output_weight, "small": small, "query_up_weight": query_up_weight, "value_up_weight": value_up_weight}


EPSILON = 1e-05
HIGHEST = lax.Precision.HIGHEST

@jax.custom_vjp
def low_rank_state(v):
    return lax.optimization_barrier(v.astype(jnp.bfloat16)).astype(jnp.float32)

@jax.custom_vjp
def low_rank_gradient(v):
    return v

def low_keep(v):
    return (low_rank_state(v), None)

def low_pass(kept, grad):
    return (grad,)

def back_keep(v):
    return (v, None)

def back_low(kept, grad):
    return (low_rank_state(grad),)
low_rank_state.defvjp(low_keep, low_pass)
low_rank_gradient.defvjp(back_keep, back_low)

def matrix_multiply(left, right):
    return jnp.dot(left, right, precision=HIGHEST, preferred_element_type=jnp.float32)

def layer_norm(value, norm_gain, norm_shift):
    average = lax.optimization_barrier(jnp.mean(value, axis=-1, keepdims=True))
    centred = value - average
    spread = lax.optimization_barrier(jnp.mean(centred * centred, axis=-1, keepdims=True))
    return centred * lax.rsqrt(spread + EPSILON) * norm_gain + norm_shift

def attend(element):
    query_rows, key_rows, value_matrix_rows = element
    length = query_rows.shape[0]
    q_heads = query_rows.reshape(length, H, HD)
    k_heads = key_rows.reshape(length, H, HD)
    v_heads = value_matrix_rows.reshape(length, H, HD)
    scores = low_rank_gradient(0.125 * jnp.einsum('qhd,khd->hqk', q_heads, k_heads, precision=HIGHEST))
    soft_probs = jax.nn.softmax(scores, axis=-1)
    context = jnp.einsum('hqk,khd->qhd', low_rank_state(soft_probs), v_heads, precision=HIGHEST)
    return context.reshape(length, H * HD)

def single_encoder_layer(hidden_state, frozen_weights, query_adapter_output, value_adapter_output):
    query_key_value_weight, attention_output_weight, feedforward_input_weight, feedforward_input_bias, feedforward_output_weight, small = frozen_weights
    rounded_input = low_rank_state(hidden_state)
    query_down_weight = low_rank_state(low_rank_gradient(matrix_multiply(rounded_input, small[:, 8:8 + ADAPTER_RANK])))
    value_down_weight = low_rank_state(low_rank_gradient(matrix_multiply(rounded_input, small[:, 8 + ADAPTER_RANK:8 + 2 * ADAPTER_RANK])))
    query_rows = low_rank_state(low_rank_gradient(matrix_multiply(rounded_input, query_key_value_weight[:, :MODEL_WIDTH]) + small[:, 0] + 2.0 * matrix_multiply(query_down_weight, low_rank_state(query_adapter_output))))
    key_rows = low_rank_state(low_rank_gradient(matrix_multiply(rounded_input, query_key_value_weight[:, MODEL_WIDTH:2 * MODEL_WIDTH])))
    value_matrix_rows = low_rank_state(low_rank_gradient(matrix_multiply(rounded_input, query_key_value_weight[:, 2 * MODEL_WIDTH:]) + small[:, 1] + 2.0 * matrix_multiply(value_down_weight, low_rank_state(value_adapter_output))))
    shaped = (query_rows.reshape(-1, LEN, MODEL_WIDTH), key_rows.reshape(-1, LEN, MODEL_WIDTH), value_matrix_rows.reshape(-1, LEN, MODEL_WIDTH))
    context = lax.map(jax.checkpoint(attend), shaped).reshape(-1, MODEL_WIDTH)
    context = low_rank_state(low_rank_gradient(context))
    attn_out = low_rank_gradient(matrix_multiply(context, attention_output_weight) + small[:, 2])
    normed = layer_norm(hidden_state + attn_out, small[:, 3], small[:, 4])
    preactivation_input = low_rank_gradient(matrix_multiply(low_rank_state(normed), feedforward_input_weight) + feedforward_input_bias)
    activated = low_rank_state(jax.nn.gelu(preactivation_input, approximate=False))
    ffn_out = low_rank_gradient(matrix_multiply(activated, feedforward_output_weight) + small[:, 5])
    return layer_norm(normed + ffn_out, small[:, 6], small[:, 7])

def reference(tokens, cotangent, positions, counts, query_key_value_weight, attention_output_weight, feedforward_input_weight, feedforward_input_bias, feedforward_output_weight, small, query_up_weight, value_up_weight):
    sequences = tokens.shape[0]
    group_size = math.gcd(sequences, max(1, 4096 // LEN))
    arrays = (query_key_value_weight, attention_output_weight, feedforward_input_weight, feedforward_input_bias, feedforward_output_weight, small)
    frozen_weights = [tuple((array[layer_index].astype(jnp.float32) for array in arrays)) for layer_index in range(ENCODER_LAYERS)]

    def forward_apply(hidden_state, query_adapter_output, value_adapter_output):
        for layer_index in range(ENCODER_LAYERS):
            hidden_state = single_encoder_layer(hidden_state, frozen_weights[layer_index], query_adapter_output[layer_index], value_adapter_output[layer_index])
        return hidden_state

    def run_group(running, element):
        group_tokens, group_cot, group_pos, group_counts = element
        input_tokens = group_tokens.astype(jnp.float32).reshape(-1, MODEL_WIDTH)
        is_live = (jnp.arange(MAXM)[None, :] < group_counts[:, None]).astype(jnp.float32)
        picks = group_pos.astype(jnp.int32)[:, :, None]

        def forward_selected_rows(hidden_state, query_adapter_output, value_adapter_output):
            layer_output = forward_apply(hidden_state, query_adapter_output, value_adapter_output)
            selected_rows = jnp.take_along_axis(layer_output.reshape(-1, LEN, MODEL_WIDTH), picks, axis=1) * is_live[:, :, None]
            return (layer_output, selected_rows)
        (layer_output, selected_rows), backward_function = jax.vjp(forward_selected_rows, input_tokens, query_up_weight, value_up_weight)
        d_inputs, query_adapter_gradient, value_adapter_gradient = backward_function((jnp.zeros_like(layer_output), group_cot.astype(jnp.float32)))
        new_running = (running[0] + query_adapter_gradient, running[1] + value_adapter_gradient)
        shaped_out = layer_output.astype(jnp.bfloat16).reshape(group_size, LEN, MODEL_WIDTH)
        return (new_running, (shaped_out, d_inputs.reshape(group_size, LEN, MODEL_WIDTH)))
    elements = (tokens.reshape(-1, group_size, LEN, MODEL_WIDTH), cotangent.reshape(-1, group_size, MAXM, MODEL_WIDTH), positions.reshape(-1, group_size, MAXM), counts.reshape(-1, group_size))
    starting_index = (jnp.zeros_like(query_up_weight), jnp.zeros_like(value_up_weight))
    (query_gradient_total, value_gradient_total), (outputs, d_inputs) = lax.scan(run_group, starting_index, elements)
    return (outputs.reshape(sequences, LEN, MODEL_WIDTH), d_inputs.reshape(sequences, LEN, MODEL_WIDTH), query_gradient_total, value_gradient_total)
```

```python
import functools

import jax
import jax.numpy as jnp
from jax import lax
from jax.experimental import pallas as pl
from jax.experimental.pallas import tpu as pltpu
from jax.sharding import PartitionSpec as P

D = 768
H = 12
HD = 64
FF = 3072
RANK = 8
LAYERS = 2
LEN = 512
MAXM = 80
EPS = 1e-05
SCALE = 0.125
BF = jnp.bfloat16
F32 = jnp.float32
AXES = ("dp", "fsdp")
INV_SQRT2 = 0.7071067811865476
INV_SQRT2PI = 0.3989422804014327
ROWS = 256


def nn(a, b):
    return lax.dot_general(a, b, (((1,), (0,)), ((), ())), preferred_element_type=F32)


def nt(a, b):
    return lax.dot_general(a, b, (((1,), (1,)), ((), ())), preferred_element_type=F32)


def tn(a, b):
    return lax.dot_general(a, b, (((0,), (0,)), ((), ())), preferred_element_type=F32)


def flat(ref):
    v = ref[...]
    return v.reshape(v.shape[0] * v.shape[1], v.shape[2])


def norm_stats(r):
    mean = jnp.mean(r, axis=-1, keepdims=True)
    c = r - mean
    rstd = lax.rsqrt(jnp.mean(c * c, axis=-1, keepdims=True) + EPS)
    return c * rstd, rstd


def norm_back(e, n, rstd, gain):
    eg = e * gain
    a = jnp.mean(eg, axis=-1, keepdims=True)
    b = jnp.mean(eg * n, axis=-1, keepdims=True)
    return rstd * (eg - a - n * b)


def params(n_steps=1):
    return pltpu.CompilerParams(
        dimension_semantics=("arbitrary",) * n_steps, vmem_limit_bytes=60 << 20
    )


def whole(shape):
    zero = (0,) * len(shape)
    return pl.BlockSpec(shape, lambda *_: zero)


def sds(shape, dtype):
    return jax.ShapeDtypeStruct(shape, dtype)


def unit_spec(packed, index):
    nb = packed.shape[0]
    rb = packed.shape[1] // 12
    return pl.BlockSpec((nb, rb, D), lambda *g: (0, index(*g), 0))


def out_spec(packed, index):
    nb = packed.shape[0]
    rb = packed.shape[1] // 12
    if nb % 4 == 0:
        return pl.BlockSpec((nb // 4, 4 * rb, D), lambda *g: (index(*g), 2, 0))
    return pl.BlockSpec((nb, rb, D), lambda *g: (0, 8 + index(*g), 0))


def qkv_kernel(x_ref, w_ref, a_ref, b_ref, bias_ref, o_ref, u_ref, wp_ref):
    j = pl.program_id(0)
    a = a_ref[...]
    wp_ref[...] = (flat(w_ref).astype(F32) + nn(a, b_ref[0])).astype(BF)
    t = x_ref.shape[0]
    for r in range(0, t, ROWS):
        x = x_ref[r : r + ROWS, :]
        o_ref[r : r + ROWS, :] = (nn(x, wp_ref[...]) + bias_ref[0]).astype(BF)

    @pl.when(j == 0)
    def _():
        u_ref[...] = nn(x_ref[...], a).astype(BF)


def qkv_call(x, packed, down, up3, bias3):
    t = x.shape[0]
    return pl.pallas_call(
        qkv_kernel,
        grid=(3,),
        in_specs=[
            whole((t, D)),
            unit_spec(packed, lambda j: j),
            whole(down.shape),
            pl.BlockSpec((1, 2 * RANK, D), lambda j: (j, 0, 0)),
            pl.BlockSpec((1, 1, D), lambda j: (j, 0, 0)),
        ],
        out_specs=[
            pl.BlockSpec((t, D), lambda j: (0, j)),
            whole((t, 2 * RANK)),
            pl.BlockSpec((D, D), lambda j: (0, j)),
        ],
        out_shape=[sds((t, 3 * D), BF), sds((t, 2 * RANK), BF), sds((D, 3 * D), BF)],
        compiler_params=params(),
        name="qkv",
    )(x, packed, down, up3, bias3)


PAIRS = H // 2


def head_spec(offset):
    return pl.BlockSpec((LEN, 2 * HD), lambda s, h: (s, offset * PAIRS + h))


def attn_kernel(q_ref, k_ref, v_ref, c_ref, z_ref):
    low = lax.broadcasted_iota(jnp.int32, (LEN, 2 * HD), 1) < HD
    q = q_ref[...] * jnp.asarray(SCALE, BF)
    k = k_ref[...]
    v = v_ref[...]
    ctx = []
    zs = []
    for h in range(2):
        mine = low if h == 0 else jnp.logical_not(low)
        s = nt(jnp.where(mine, q, jnp.zeros_like(q)), k)
        m = jnp.max(s, axis=-1, keepdims=True)
        p = jnp.exp(s - m).astype(BF)
        o = nn(p, jnp.where(mine, v, jnp.ones_like(v)))
        total = pltpu.roll(o, HD, 1)
        ctx.append(o / total)
        zs.append(m + jnp.log(total))
    c_ref[...] = jnp.where(low, ctx[0], ctx[1]).astype(BF)
    z_ref[...] = jnp.where(low, zs[0], zs[1])


def attn_call(qkv):
    t = qkv.shape[0]
    return pl.pallas_call(
        attn_kernel,
        grid=(t // LEN, PAIRS),
        in_specs=[head_spec(0), head_spec(1), head_spec(2)],
        out_specs=[head_spec(0), head_spec(0)],
        out_shape=[sds((t, D), BF), sds((t, D), F32)],
        compiler_params=params(2),
        name="attn_fwd",
    )(qkv, qkv, qkv)


def ffn_kernel(keep, h_ref, c_ref, wo_ref, win_ref, wout_ref, par_ref, fb_ref, *rest):
    if keep:
        hb_ref, n1_ref, s1_ref, n2_ref, s2_ref, ho_ref, gp_ref, h1_ref, acc_ref = rest
    else:
        hb_ref, n1_ref, s1_ref, n2_ref, s2_ref, h1_ref, acc_ref = rest
    j = pl.program_id(0)
    t = h_ref.shape[0]

    @pl.when(j == 0)
    def _():
        wo = flat(wo_ref)
        for r in range(0, t, ROWS):
            w = slice(r, r + ROWS)
            r1 = h_ref[w, :].astype(F32) + (nn(c_ref[w, :], wo) + par_ref[2:3, :])
            n1, s1 = norm_stats(r1)
            n1_ref[w, :] = n1.astype(BF)
            s1_ref[w, :] = s1
            h1 = n1 * par_ref[3:4, :] + par_ref[4:5, :]
            h1_ref[w, :] = h1.astype(BF)
            acc_ref[w, :] = h1 + par_ref[5:6, :]

    win = flat(win_ref)
    wout = flat(wout_ref)
    for r in range(0, t, ROWS):
        w = slice(r, r + ROWS)
        f = nn(h1_ref[w, :], win) + fb_ref[...]
        cdf = 0.5 + 0.5 * lax.erf(f * INV_SQRT2)
        act = (f * cdf).astype(BF)
        if keep:
            gp_ref[w, :] = (cdf + f * (INV_SQRT2PI * jnp.exp(-0.5 * (f * f)))).astype(BF)
        acc_ref[w, :] += nn(act, wout)

    @pl.when(j == 3)
    def _():
        for r in range(0, t, ROWS):
            w = slice(r, r + ROWS)
            n2, s2 = norm_stats(acc_ref[w, :])
            n2_ref[w, :] = n2.astype(BF)
            s2_ref[w, :] = s2
            h = n2 * par_ref[6:7, :] + par_ref[7:8, :]
            hb_ref[w, :] = h.astype(BF)
            if keep:
                ho_ref[w, :] = h


def ffn_call(h, ctx, packed, par, fb, keep):
    t = h.shape[0]
    out_specs = [whole((t, D)), whole((t, D)), whole((t, 1)), whole((t, D)), whole((t, 1))]
    out_shape = [sds((t, D), BF), sds((t, D), BF), sds((t, 1), F32), sds((t, D), BF), sds((t, 1), F32)]
    if keep:
        out_specs += [whole((t, D)), pl.BlockSpec((t, D), lambda j: (0, j))]
        out_shape += [sds((t, D), F32), sds((t, FF), BF)]
    return pl.pallas_call(
        functools.partial(ffn_kernel, keep),
        grid=(4,),
        in_specs=[
            whole((t, D)),
            whole((t, D)),
            unit_spec(packed, lambda j: 3),
            unit_spec(packed, lambda j: 4 + j),
            out_spec(packed, lambda j: j),
            whole(par.shape),
            pl.BlockSpec((1, D), lambda j: (0, j)),
        ],
        out_specs=out_specs,
        out_shape=out_shape,
        scratch_shapes=[pltpu.VMEM((t, D), BF), pltpu.VMEM((t, D), F32)],
        compiler_params=params(),
        name="ffn_fwd",
    )(h, ctx, packed, packed, packed, par, fb)


def pick(pos_ref, s, dtype):
    column = pos_ref[s * MAXM : (s + 1) * MAXM, :]
    return (lax.broadcasted_iota(jnp.int32, (MAXM, LEN), 1) == column).astype(dtype)


def ffn_pick_kernel(
    seqs, cnt_ref, cot_ref, pos_ref, n1_ref, s1_ref, n2_ref, s2_ref, wo_ref, win_ref, wout_ref, par_ref, fb_ref,
    dr1_ref, dctx_ref, h1_ref, d2_ref, n1s_ref, s1s_ref, acc_ref,
):
    j = pl.program_id(0)

    @pl.when(j == 0)
    def _():
        for s in range(seqs):
            w = slice(s * LEN, (s + 1) * LEN)
            m = slice(s * MAXM, (s + 1) * MAXM)
            onehot = pick(pos_ref, s, BF)
            onehot_f = pick(pos_ref, s, F32)

            def take(v):
                return lax.dot_general(
                    onehot_f, v, (((1,), (0,)), ((), ())),
                    precision=lax.Precision.HIGHEST, preferred_element_type=F32,
                )

            n1 = nn(onehot, n1_ref[w, :])
            n2 = nn(onehot, n2_ref[w, :])
            live = lax.broadcasted_iota(jnp.int32, (MAXM, D), 0) < cnt_ref[s]
            e = jnp.where(live, cot_ref[m, :].astype(F32), 0.0)
            d2 = norm_back(e, n2, take(s2_ref[w, :]), par_ref[6:7, :])
            n1s_ref[m, :] = n1
            s1s_ref[m, :] = take(s1_ref[w, :])
            h1_ref[m, :] = (n1 * par_ref[3:4, :] + par_ref[4:5, :]).astype(BF)
            d2_ref[m, :] = d2.astype(BF)
            acc_ref[m, :] = d2

    win = flat(win_ref)
    f = nn(h1_ref[...], win) + fb_ref[...]
    cdf = 0.5 + 0.5 * lax.erf(f * INV_SQRT2)
    gp = cdf + f * (INV_SQRT2PI * jnp.exp(-0.5 * (f * f)))
    df = (nt(d2_ref[...], flat(wout_ref)) * gp).astype(BF)
    acc_ref[...] += nt(df, win)

    @pl.when(j == 3)
    def _():
        d1 = norm_back(acc_ref[...], n1s_ref[...], s1s_ref[...], par_ref[3:4, :])
        dr1_ref[...] = d1
        dctx_ref[...] = nt(d1.astype(BF), flat(wo_ref)).astype(BF)


def ffn_pick_call(cot, pos, counts, n1, s1, n2, s2, packed, par, fb):
    t = n1.shape[0]
    seqs = t // LEN
    m = seqs * MAXM
    return pl.pallas_call(
        functools.partial(ffn_pick_kernel, seqs),
        grid=(4,),
        in_specs=[
            pl.BlockSpec(memory_space=pltpu.SMEM),
            whole((m, D)),
            whole((m, 1)),
            whole((t, D)),
            whole((t, 1)),
            whole((t, D)),
            whole((t, 1)),
            unit_spec(packed, lambda j: 3),
            unit_spec(packed, lambda j: 4 + j),
            out_spec(packed, lambda j: j),
            whole(par.shape),
            pl.BlockSpec((1, D), lambda j: (0, j)),
        ],
        out_specs=[whole((m, D)), whole((m, D))],
        out_shape=[sds((m, D), F32), sds((m, D), BF)],
        scratch_shapes=[
            pltpu.VMEM((m, D), BF),
            pltpu.VMEM((m, D), BF),
            pltpu.VMEM((m, D), F32),
            pltpu.VMEM((m, 1), F32),
            pltpu.VMEM((m, D), F32),
        ],
        compiler_params=params(),
        name="ffn_bwd_rows",
    )(counts, cot, pos, n1, s1, n2, s2, packed, packed, packed, par, fb)


def attn_pick_kernel(q_ref, k_ref, v_ref, g_ref, pos_ref, u_ref, dq_ref, dk_ref, dv_ref, gq_ref, gv_ref):
    low = lax.broadcasted_iota(jnp.int32, (LEN, 2 * HD), 1) < HD
    low_m = lax.broadcasted_iota(jnp.int32, (MAXM, 2 * HD), 1) < HD
    onehot = pick(pos_ref, 0, BF)
    qs = nn(onehot, q_ref[...]).astype(BF)
    qsc = qs * jnp.asarray(SCALE, BF)
    us = nn(onehot, u_ref[...]).astype(BF)
    k = k_ref[...]
    v = v_ref[...]
    g = g_ref[...]
    dqs, dks, dvs = [], [], []
    for h in range(2):
        mine = low_m if h == 0 else jnp.logical_not(low_m)
        s = nt(jnp.where(mine, qsc, jnp.zeros_like(qsc)), k)
        p = jnp.exp(s - jnp.max(s, axis=-1, keepdims=True))
        p = p * (1.0 / jnp.sum(p, axis=-1, keepdims=True))
        dp = nt(jnp.where(mine, g, jnp.zeros_like(g)), v)
        ds = (p * (dp - jnp.sum(p * dp, axis=-1, keepdims=True))).astype(BF)
        dqs.append(nn(ds, k))
        dks.append(tn(ds, qs))
        dvs.append(tn(p.astype(BF), g))
    dq = (jnp.where(low_m, dqs[0], dqs[1]) * SCALE).astype(BF)
    dv = jnp.where(low, dvs[0], dvs[1]).astype(BF)
    dq_ref[...] = dq
    dk_ref[...] = (jnp.where(low, dks[0], dks[1]) * SCALE).astype(BF)
    dv_ref[...] = dv
    gq_ref[0] = 2.0 * tn(us, dq)
    gv_ref[0] = 2.0 * tn(u_ref[...], dv)


def attn_pick_call(qkv, g, pos, u):
    t = qkv.shape[0]
    seqs = t // LEN
    grads = pl.BlockSpec((1, 2 * RANK, 2 * HD), lambda s, h: (s, 0, h))
    rows = pl.BlockSpec((MAXM, 2 * HD), lambda s, h: (s, h))
    return pl.pallas_call(
        attn_pick_kernel,
        grid=(seqs, PAIRS),
        in_specs=[
            head_spec(0),
            head_spec(1),
            head_spec(2),
            rows,
            pl.BlockSpec((MAXM, 1), lambda s, h: (s, 0)),
            pl.BlockSpec((LEN, 2 * RANK), lambda s, h: (s, 0)),
        ],
        out_specs=[rows, head_spec(0), head_spec(0), grads, grads],
        out_shape=[
            sds((seqs * MAXM, D), BF),
            sds((t, D), BF),
            sds((t, D), BF),
            sds((seqs, 2 * RANK, D), F32),
            sds((seqs, 2 * RANK, D), F32),
        ],
        compiler_params=params(2),
        name="attn_bwd_rows",
    )(qkv, qkv, qkv, g, pos, u)


def dh_pick_kernel(dr1_ref, dq_ref, dk_ref, dv_ref, pos_ref, w_ref, o_ref):
    rows = dr1_ref[...] + nt(dq_ref[...], w_ref[:, 0:D])
    high = rows.astype(BF)
    rest = (rows - high.astype(F32)).astype(BF)
    onehot = (lax.broadcasted_iota(jnp.int32, (LEN, MAXM), 0) == pos_ref[0]).astype(BF)
    o_ref[...] = (
        nt(dk_ref[...], w_ref[:, D : 2 * D])
        + nt(dv_ref[...], w_ref[:, 2 * D : 3 * D])
        + nn(onehot, high)
        + nn(onehot, rest)
    )


def dh_pick_call(dr1, dq, dk, dv, pos_row, wp):
    t = dk.shape[0]
    rows = pl.BlockSpec((MAXM, D), lambda s: (s, 0))
    block = pl.BlockSpec((LEN, D), lambda s: (s, 0))
    return pl.pallas_call(
        dh_pick_kernel,
        grid=(t // LEN,),
        in_specs=[rows, rows, block, block, pl.BlockSpec((1, 1, MAXM), lambda s: (s, 0, 0)), whole((D, 3 * D))],
        out_specs=block,
        out_shape=sds((t, D), F32),
        compiler_params=params(),
        name="dh_rows",
    )(dr1, dq, dk, dv, pos_row, wp)


def ffn_back_kernel(e_ref, n1_ref, s1_ref, n2_ref, s2_ref, gp_ref, wo_ref, win_ref, wout_ref, par_ref,
                    dr1_ref, dctx_ref, d2_ref, acc_ref):
    j = pl.program_id(0)
    t = e_ref.shape[0]

    @pl.when(j == 0)
    def _():
        for r in range(0, t, ROWS):
            w = slice(r, r + ROWS)
            d2 = norm_back(e_ref[w, :], n2_ref[w, :].astype(F32), s2_ref[w, :], par_ref[6:7, :])
            d2_ref[w, :] = d2.astype(BF)
            acc_ref[w, :] = d2

    win = flat(win_ref)
    wout = flat(wout_ref)
    for r in range(0, t, ROWS):
        w = slice(r, r + ROWS)
        df = (nt(d2_ref[w, :], wout) * gp_ref[w, :].astype(F32)).astype(BF)
        acc_ref[w, :] += nt(df, win)

    @pl.when(j == 3)
    def _():
        wo = flat(wo_ref)
        for r in range(0, t, ROWS):
            w = slice(r, r + ROWS)
            d1 = norm_back(acc_ref[w, :], n1_ref[w, :].astype(F32), s1_ref[w, :], par_ref[3:4, :])
            dr1_ref[w, :] = d1
            dctx_ref[w, :] = nt(d1.astype(BF), wo).astype(BF)


def ffn_back_call(e, n1, s1, n2, s2, gp, packed, par):
    t = e.shape[0]
    return pl.pallas_call(
        ffn_back_kernel,
        grid=(4,),
        in_specs=[
            whole((t, D)),
            whole((t, D)),
            whole((t, 1)),
            whole((t, D)),
            whole((t, 1)),
            pl.BlockSpec((t, D), lambda j: (0, j)),
            unit_spec(packed, lambda j: 3),
            unit_spec(packed, lambda j: 4 + j),
            out_spec(packed, lambda j: j),
            whole(par.shape),
        ],
        out_specs=[whole((t, D)), whole((t, D))],
        out_shape=[sds((t, D), F32), sds((t, D), BF)],
        scratch_shapes=[pltpu.VMEM((t, D), BF), pltpu.VMEM((t, D), F32)],
        compiler_params=params(),
        name="ffn_bwd",
    )(e, n1, s1, n2, s2, gp, packed, packed, packed, par)


def attn_back_kernel(q_ref, k_ref, v_ref, g_ref, z_ref, u_ref, dq_ref, dk_ref, dv_ref, gq_ref, gv_ref):
    low = lax.broadcasted_iota(jnp.int32, (LEN, 2 * HD), 1) < HD
    q = q_ref[...]
    qsc = q * jnp.asarray(SCALE, BF)
    k = k_ref[...]
    v = v_ref[...]
    g = g_ref[...]
    zt = z_ref[...].T
    kt = k.T
    dqs, dks, dvs = [], [], []
    for h in range(2):
        mine = low if h == 0 else jnp.logical_not(low)
        st = nt(k, jnp.where(mine, qsc, jnp.zeros_like(q)))
        pt = jnp.exp(st - zt[h * HD : h * HD + 1, :])
        dpt = nt(v, jnp.where(mine, g, jnp.zeros_like(g)))
        ds = (pt * (dpt - jnp.sum(pt * dpt, axis=0, keepdims=True))).astype(BF)
        dvs.append(nn(pt.astype(BF), g))
        dks.append(nn(ds, q))
        dqs.append(nn(kt[h * HD : (h + 1) * HD, :], ds))
    dq = (jnp.concatenate(dqs, axis=0).T * SCALE).astype(BF)
    dv = jnp.where(low, dvs[0], dvs[1]).astype(BF)
    dq_ref[...] = dq
    dk_ref[...] = (jnp.where(low, dks[0], dks[1]) * SCALE).astype(BF)
    dv_ref[...] = dv
    gq_ref[0] = 2.0 * tn(u_ref[...], dq)
    gv_ref[0] = 2.0 * tn(u_ref[...], dv)


def attn_back_call(qkv, g, z, u):
    t = qkv.shape[0]
    seqs = t // LEN
    grads = pl.BlockSpec((1, 2 * RANK, 2 * HD), lambda s, h: (s, 0, h))
    return pl.pallas_call(
        attn_back_kernel,
        grid=(seqs, PAIRS),
        in_specs=[
            head_spec(0),
            head_spec(1),
            head_spec(2),
            head_spec(0),
            head_spec(0),
            pl.BlockSpec((LEN, 2 * RANK), lambda s, h: (s, 0)),
        ],
        out_specs=[head_spec(0), head_spec(0), head_spec(0), grads, grads],
        out_shape=[sds((t, D), BF)] * 3 + [sds((seqs, 2 * RANK, D), F32)] * 2,
        compiler_params=params(2),
        name="attn_bwd",
    )(qkv, qkv, qkv, g, z, u)


def dh_kernel(dr1_ref, dq_ref, dk_ref, dv_ref, w_ref, o_ref):
    o_ref[...] = (
        dr1_ref[...]
        + nt(dq_ref[...], w_ref[:, 0:D])
        + nt(dk_ref[...], w_ref[:, D : 2 * D])
        + nt(dv_ref[...], w_ref[:, 2 * D : 3 * D])
    )


def dh_call(dr1, dq, dk, dv, wp):
    t = dk.shape[0]
    block = pl.BlockSpec((ROWS, D), lambda i: (i, 0))
    return pl.pallas_call(
        dh_kernel,
        grid=(t // ROWS,),
        in_specs=[block, block, block, block, whole((D, 3 * D))],
        out_specs=block,
        out_shape=sds((t, D), F32),
        compiler_params=params(),
        name="dh",
    )(dr1, dq, dk, dv, wp)


def network(tokens, cotangent, positions, counts, packed, smalls, biases, query_up, value_up):
    seqs = tokens.shape[0]
    x = tokens.reshape(seqs * LEN, D)
    pos_col = positions.reshape(seqs * MAXM, 1)
    pos_row = positions.reshape(seqs, 1, MAXM)
    cot = cotangent.reshape(seqs * MAXM, D)
    h = x
    saved = []
    for layer in range(LAYERS):
        small = smalls[layer]
        par = small.astype(F32).T
        down = small[:, 8 : 8 + 2 * RANK]
        zero = jnp.zeros((RANK, D), BF)
        up3 = jnp.stack(
            [
                jnp.concatenate([2.0 * query_up[layer].astype(BF), zero]),
                jnp.concatenate([zero, zero]),
                jnp.concatenate([zero, 2.0 * value_up[layer].astype(BF)]),
            ]
        )
        bias3 = jnp.stack([par[0:1], jnp.zeros((1, D), F32), par[1:2]])
        keep = layer < LAYERS - 1
        qkv, u, wp = qkv_call(x, packed[layer], down, up3, bias3)
        ctx, z = attn_call(qkv)
        outs = ffn_call(h, ctx, packed[layer], par, biases[layer], keep)
        x, n1, s1, n2, s2 = outs[:5]
        gp = None
        if keep:
            h, gp = outs[5:]
        saved.append((qkv, u, wp, z, n1, s1, n2, s2, gp, par))
    activations = x.reshape(tokens.shape)

    grads = [None] * LAYERS
    qkv, u, wp, z, n1, s1, n2, s2, gp, par = saved[-1]
    dr1, dctx = ffn_pick_call(
        cot, pos_col, counts, n1, s1, n2, s2, packed[-1], par, biases[-1]
    )
    dq, dk, dv, gq, gv = attn_pick_call(qkv, dctx, pos_col, u)
    grads[-1] = (gq, gv)
    e = dh_pick_call(dr1, dq, dk, dv, pos_row, wp)
    for layer in reversed(range(LAYERS - 1)):
        qkv, u, wp, z, n1, s1, n2, s2, gp, par = saved[layer]
        dr1, dctx = ffn_back_call(e, n1, s1, n2, s2, gp, packed[layer], par)
        dq, dk, dv, gq, gv = attn_back_call(qkv, dctx, z, u)
        grads[layer] = (gq, gv)
        e = dh_call(dr1, dq, dk, dv, wp)
    out = []
    for gq, gv in grads:
        out.append(
            jnp.concatenate([jnp.sum(gq, 0)[:RANK], jnp.sum(gv, 0)[RANK:]])
        )
    return activations, e.reshape(tokens.shape), out


def column_blocks(w, n):
    return [w[:, i * D : (i + 1) * D] for i in range(n)]


def on_device(
    tokens, cotangent, positions, counts, w_qkv, w_o, w_in, b_in, w_out, small, query_up, value_up
):
    packed, smalls, biases = [], [], []
    for layer in range(LAYERS):
        shard = jnp.concatenate(
            column_blocks(w_qkv[layer], 3) + [w_o[layer]] + column_blocks(w_in[layer], 4) + [w_out[layer]]
        )
        rb = w_o.shape[1]
        if rb % 8 == 0:
            packed.append(lax.all_gather(shard, AXES, axis=0, tiled=False))
        else:
            g = lax.all_gather(shard, AXES, axis=0, tiled=False)
            units = [g[:, i * rb : (i + 1) * rb].reshape(1, D, D) for i in range(8)]
            units.append(g[:, 8 * rb :].reshape(1, FF, D))
            packed.append(jnp.concatenate(units, axis=1))
    tiny = jnp.concatenate(
        [small.reshape(-1), b_in.reshape(-1)]
    )
    tiny = lax.all_gather(tiny, AXES, axis=0, tiled=False)
    n = tiny.shape[0]
    cut = small.size
    sm = tiny[:, :cut].reshape(n, LAYERS, -1, small.shape[2])
    bi = tiny[:, cut:].reshape(n, LAYERS, -1)
    for layer in range(LAYERS):
        smalls.append(sm[:, layer].reshape(D, small.shape[2]))
        biases.append(bi[:, layer].reshape(1, FF).astype(F32))
    activations, d_tokens, grads = network(
        tokens, cotangent, positions, counts, packed, smalls, biases, query_up, value_up
    )
    g = lax.psum(jnp.stack(grads), AXES)
    return activations, d_tokens, g[:, :RANK], g[:, RANK:]


def solution(mesh):
    both = P(AXES, None, None)
    mid = P(None, AXES, None)
    in_specs = (both, both, P(AXES, None), P(AXES), mid, mid, mid, P(None, AXES), mid, mid, P(), P())
    out_specs = (both, both, P(), P())
    return jax.shard_map(on_device, mesh=mesh, in_specs=in_specs, out_specs=out_specs, check_vma=False)
```

```python
import functools

import jax
import jax.numpy as jnp
from jax import lax
from jax.experimental import pallas as pl
from jax.experimental.pallas import tpu as pltpu
from jax.sharding import PartitionSpec as P

D = 768
H = 12
HD = 64
FF = 3072
RANK = 8
LAYERS = 2
LEN = 512
MAXM = 80
EPS = 1e-05
SCALE = 0.125
BF = jnp.bfloat16
F32 = jnp.float32
AXES = ("dp", "fsdp")
INV_SQRT2 = 0.7071067811865476
INV_SQRT2PI = 0.3989422804014327
ROWS = 256


def nn(a, b):
    return lax.dot_general(a, b, (((1,), (0,)), ((), ())), preferred_element_type=F32)


def nt(a, b):
    return lax.dot_general(a, b, (((1,), (1,)), ((), ())), preferred_element_type=F32)


def tn(a, b):
    return lax.dot_general(a, b, (((0,), (0,)), ((), ())), preferred_element_type=F32)


def flat(ref):
    v = ref[...]
    return v.reshape(v.shape[0] * v.shape[1], v.shape[2])


def norm_stats(r):
    mean = jnp.mean(r, axis=-1, keepdims=True)
    c = r - mean
    rstd = lax.rsqrt(jnp.mean(c * c, axis=-1, keepdims=True) + EPS)
    return c * rstd, rstd


def norm_back(e, n, rstd, gain):
    eg = e * gain
    a = jnp.mean(eg, axis=-1, keepdims=True)
    b = jnp.mean(eg * n, axis=-1, keepdims=True)
    return rstd * (eg - a - n * b)


def params(n_steps=1):
    return pltpu.CompilerParams(
        dimension_semantics=("arbitrary",) * n_steps, vmem_limit_bytes=60 << 20
    )


def whole(shape):
    zero = (0,) * len(shape)
    return pl.BlockSpec(shape, lambda *_: zero)


def sds(shape, dtype):
    return jax.ShapeDtypeStruct(shape, dtype)


def unit_spec(weight, index):
    packed, base = weight
    nb = packed.shape[0]
    return pl.BlockSpec((nb, D // nb, D), lambda *g: (0, base + index(*g), 0))


def out_spec(weight, index):
    packed, base = weight
    nb = packed.shape[0]
    rb = D // nb
    if nb % 4 == 0:
        return pl.BlockSpec((nb // 4, 4 * rb, D), lambda *g: (index(*g), base, 0))
    return pl.BlockSpec((nb, rb, D), lambda *g: (0, 4 * base + index(*g), 0))


def qkv_kernel(x_ref, w_ref, a_ref, b_ref, bias_ref, o_ref, u_ref, wp_ref):
    j = pl.program_id(0)
    a = a_ref[...]
    wp_ref[...] = (flat(w_ref).astype(F32) + nn(a, b_ref[0])).astype(BF)
    t = x_ref.shape[0]
    for r in range(0, t, ROWS):
        x = x_ref[r : r + ROWS, :]
        o_ref[r : r + ROWS, :] = (nn(x, wp_ref[...]) + bias_ref[0]).astype(BF)

    @pl.when(j == 0)
    def _():
        u_ref[...] = nn(x_ref[...], a).astype(BF)


def qkv_call(x, weights, down, up3, bias3):
    t = x.shape[0]
    return pl.pallas_call(
        qkv_kernel,
        grid=(3,),
        in_specs=[
            whole((t, D)),
            unit_spec(weights["qkv"], lambda j: j),
            whole(down.shape),
            pl.BlockSpec((1, 2 * RANK, D), lambda j: (j, 0, 0)),
            pl.BlockSpec((1, 1, D), lambda j: (j, 0, 0)),
        ],
        out_specs=[
            pl.BlockSpec((t, D), lambda j: (0, j)),
            whole((t, 2 * RANK)),
            pl.BlockSpec((D, D), lambda j: (0, j)),
        ],
        out_shape=[sds((t, 3 * D), BF), sds((t, 2 * RANK), BF), sds((D, 3 * D), BF)],
        compiler_params=params(),
        name="qkv",
    )(x, weights["qkv"][0], down, up3, bias3)


PAIRS = H // 2


def head_spec(offset):
    return pl.BlockSpec((LEN, 2 * HD), lambda s, h: (s, offset * PAIRS + h))


def attn_kernel(q_ref, k_ref, v_ref, c_ref, z_ref):
    low = lax.broadcasted_iota(jnp.int32, (LEN, 2 * HD), 1) < HD
    q = q_ref[...] * jnp.asarray(SCALE, BF)
    k = k_ref[...]
    v = v_ref[...]
    ctx = []
    zs = []
    for h in range(2):
        mine = low if h == 0 else jnp.logical_not(low)
        s = nt(jnp.where(mine, q, jnp.zeros_like(q)), k)
        m = jnp.max(s, axis=-1, keepdims=True)
        p = jnp.exp(s - m).astype(BF)
        o = nn(p, jnp.where(mine, v, jnp.ones_like(v)))
        total = pltpu.roll(o, HD, 1)
        ctx.append(o / total)
        zs.append(m + jnp.log(total))
    c_ref[...] = jnp.where(low, ctx[0], ctx[1]).astype(BF)
    z_ref[...] = jnp.where(low, zs[0], zs[1])


def attn_call(qkv):
    t = qkv.shape[0]
    return pl.pallas_call(
        attn_kernel,
        grid=(t // LEN, PAIRS),
        in_specs=[head_spec(0), head_spec(1), head_spec(2)],
        out_specs=[head_spec(0), head_spec(0)],
        out_shape=[sds((t, D), BF), sds((t, D), F32)],
        compiler_params=params(2),
        name="attn_fwd",
    )(qkv, qkv, qkv)


def ffn_kernel(keep, h_ref, c_ref, wo_ref, win_ref, wout_ref, par_ref, fb_ref, *rest):
    if keep:
        hb_ref, n1_ref, s1_ref, n2_ref, s2_ref, ho_ref, gp_ref, h1_ref, acc_ref = rest
    else:
        hb_ref, n1_ref, s1_ref, n2_ref, s2_ref, h1_ref, acc_ref = rest
    j = pl.program_id(0)
    t = h_ref.shape[0]

    @pl.when(j == 0)
    def _():
        wo = flat(wo_ref)
        for r in range(0, t, ROWS):
            w = slice(r, r + ROWS)
            r1 = h_ref[w, :].astype(F32) + (nn(c_ref[w, :], wo) + par_ref[2:3, :])
            n1, s1 = norm_stats(r1)
            n1_ref[w, :] = n1.astype(BF)
            s1_ref[w, :] = s1
            h1 = n1 * par_ref[3:4, :] + par_ref[4:5, :]
            h1_ref[w, :] = h1.astype(BF)
            acc_ref[w, :] = h1 + par_ref[5:6, :]

    win = flat(win_ref)
    wout = flat(wout_ref)
    for r in range(0, t, ROWS):
        w = slice(r, r + ROWS)
        f = nn(h1_ref[w, :], win) + fb_ref[...]
        cdf = 0.5 + 0.5 * lax.erf(f * INV_SQRT2)
        act = (f * cdf).astype(BF)
        if keep:
            gp_ref[w, :] = (cdf + f * (INV_SQRT2PI * jnp.exp(-0.5 * (f * f)))).astype(BF)
        acc_ref[w, :] += nn(act, wout)

    @pl.when(j == 3)
    def _():
        for r in range(0, t, ROWS):
            w = slice(r, r + ROWS)
            n2, s2 = norm_stats(acc_ref[w, :])
            n2_ref[w, :] = n2.astype(BF)
            s2_ref[w, :] = s2
            h = n2 * par_ref[6:7, :] + par_ref[7:8, :]
            hb_ref[w, :] = h.astype(BF)
            if keep:
                ho_ref[w, :] = h


def ffn_call(h, ctx, weights, par, fb, keep):
    t = h.shape[0]
    out_specs = [whole((t, D)), whole((t, D)), whole((t, 1)), whole((t, D)), whole((t, 1))]
    out_shape = [sds((t, D), BF), sds((t, D), BF), sds((t, 1), F32), sds((t, D), BF), sds((t, 1), F32)]
    if keep:
        out_specs += [whole((t, D)), pl.BlockSpec((t, D), lambda j: (0, j))]
        out_shape += [sds((t, D), F32), sds((t, FF), BF)]
    return pl.pallas_call(
        functools.partial(ffn_kernel, keep),
        grid=(4,),
        in_specs=[
            whole((t, D)),
            whole((t, D)),
            unit_spec(weights["o"], lambda j: 0),
            unit_spec(weights["in"], lambda j: j),
            out_spec(weights["out"], lambda j: j),
            whole(par.shape),
            pl.BlockSpec((1, D), lambda j: (0, j)),
        ],
        out_specs=out_specs,
        out_shape=out_shape,
        scratch_shapes=[pltpu.VMEM((t, D), BF), pltpu.VMEM((t, D), F32)],
        compiler_params=params(),
        name="ffn_fwd",
    )(h, ctx, weights["o"][0], weights["in"][0], weights["out"][0], par, fb)


def pick(pos_ref, s, dtype):
    column = pos_ref[s * MAXM : (s + 1) * MAXM, :]
    return (lax.broadcasted_iota(jnp.int32, (MAXM, LEN), 1) == column).astype(dtype)


def ffn_pick_kernel(
    seqs, cnt_ref, cot_ref, pos_ref, n1_ref, s1_ref, n2_ref, s2_ref, wo_ref, win_ref, wout_ref, par_ref, fb_ref,
    dr1_ref, dctx_ref, h1_ref, d2_ref, n1s_ref, s1s_ref, acc_ref,
):
    j = pl.program_id(0)

    @pl.when(j == 0)
    def _():
        for s in range(seqs):
            w = slice(s * LEN, (s + 1) * LEN)
            m = slice(s * MAXM, (s + 1) * MAXM)
            onehot = pick(pos_ref, s, BF)
            onehot_f = pick(pos_ref, s, F32)

            def take(v):
                return lax.dot_general(
                    onehot_f, v, (((1,), (0,)), ((), ())),
                    precision=lax.Precision.HIGHEST, preferred_element_type=F32,
                )

            n1 = nn(onehot, n1_ref[w, :])
            n2 = nn(onehot, n2_ref[w, :])
            live = lax.broadcasted_iota(jnp.int32, (MAXM, D), 0) < cnt_ref[s]
            e = jnp.where(live, cot_ref[m, :].astype(F32), 0.0)
            d2 = norm_back(e, n2, take(s2_ref[w, :]), par_ref[6:7, :])
            n1s_ref[m, :] = n1
            s1s_ref[m, :] = take(s1_ref[w, :])
            h1_ref[m, :] = (n1 * par_ref[3:4, :] + par_ref[4:5, :]).astype(BF)
            d2_ref[m, :] = d2.astype(BF)
            acc_ref[m, :] = d2

    win = flat(win_ref)
    f = nn(h1_ref[...], win) + fb_ref[...]
    cdf = 0.5 + 0.5 * lax.erf(f * INV_SQRT2)
    gp = cdf + f * (INV_SQRT2PI * jnp.exp(-0.5 * (f * f)))
    df = (nt(d2_ref[...], flat(wout_ref)) * gp).astype(BF)
    acc_ref[...] += nt(df, win)

    @pl.when(j == 3)
    def _():
        d1 = norm_back(acc_ref[...], n1s_ref[...], s1s_ref[...], par_ref[3:4, :])
        dr1_ref[...] = d1
        dctx_ref[...] = nt(d1.astype(BF), flat(wo_ref)).astype(BF)


def ffn_pick_call(cot, pos, counts, n1, s1, n2, s2, weights, par, fb):
    t = n1.shape[0]
    seqs = t // LEN
    m = seqs * MAXM
    return pl.pallas_call(
        functools.partial(ffn_pick_kernel, seqs),
        grid=(4,),
        in_specs=[
            pl.BlockSpec(memory_space=pltpu.SMEM),
            whole((m, D)),
            whole((m, 1)),
            whole((t, D)),
            whole((t, 1)),
            whole((t, D)),
            whole((t, 1)),
            unit_spec(weights["o"], lambda j: 0),
            unit_spec(weights["in"], lambda j: j),
            out_spec(weights["out"], lambda j: j),
            whole(par.shape),
            pl.BlockSpec((1, D), lambda j: (0, j)),
        ],
        out_specs=[whole((m, D)), whole((m, D))],
        out_shape=[sds((m, D), F32), sds((m, D), BF)],
        scratch_shapes=[
            pltpu.VMEM((m, D), BF),
            pltpu.VMEM((m, D), BF),
            pltpu.VMEM((m, D), F32),
            pltpu.VMEM((m, 1), F32),
            pltpu.VMEM((m, D), F32),
        ],
        compiler_params=params(),
        name="ffn_bwd_rows",
    )(counts, cot, pos, n1, s1, n2, s2, weights["o"][0], weights["in"][0], weights["out"][0], par, fb)


def attn_pick_kernel(q_ref, k_ref, v_ref, g_ref, pos_ref, u_ref, dq_ref, dk_ref, dv_ref, gq_ref, gv_ref):
    low = lax.broadcasted_iota(jnp.int32, (LEN, 2 * HD), 1) < HD
    low_m = lax.broadcasted_iota(jnp.int32, (MAXM, 2 * HD), 1) < HD
    onehot = pick(pos_ref, 0, BF)
    qs = nn(onehot, q_ref[...]).astype(BF)
    qsc = qs * jnp.asarray(SCALE, BF)
    us = nn(onehot, u_ref[...]).astype(BF)
    k = k_ref[...]
    v = v_ref[...]
    g = g_ref[...]
    dqs, dks, dvs = [], [], []
    for h in range(2):
        mine = low_m if h == 0 else jnp.logical_not(low_m)
        s = nt(jnp.where(mine, qsc, jnp.zeros_like(qsc)), k)
        p = jnp.exp(s - jnp.max(s, axis=-1, keepdims=True))
        p = p * (1.0 / jnp.sum(p, axis=-1, keepdims=True))
        dp = nt(jnp.where(mine, g, jnp.zeros_like(g)), v)
        ds = (p * (dp - jnp.sum(p * dp, axis=-1, keepdims=True))).astype(BF)
        dqs.append(nn(ds, k))
        dks.append(tn(ds, qs))
        dvs.append(tn(p.astype(BF), g))
    dq = (jnp.where(low_m, dqs[0], dqs[1]) * SCALE).astype(BF)
    dv = jnp.where(low, dvs[0], dvs[1]).astype(BF)
    dq_ref[...] = dq
    dk_ref[...] = (jnp.where(low, dks[0], dks[1]) * SCALE).astype(BF)
    dv_ref[...] = dv
    gq_ref[0] = 2.0 * tn(us, dq)
    gv_ref[0] = 2.0 * tn(u_ref[...], dv)


def attn_pick_call(qkv, g, pos, u):
    t = qkv.shape[0]
    seqs = t // LEN
    grads = pl.BlockSpec((1, 2 * RANK, 2 * HD), lambda s, h: (s, 0, h))
    rows = pl.BlockSpec((MAXM, 2 * HD), lambda s, h: (s, h))
    return pl.pallas_call(
        attn_pick_kernel,
        grid=(seqs, PAIRS),
        in_specs=[
            head_spec(0),
            head_spec(1),
            head_spec(2),
            rows,
            pl.BlockSpec((MAXM, 1), lambda s, h: (s, 0)),
            pl.BlockSpec((LEN, 2 * RANK), lambda s, h: (s, 0)),
        ],
        out_specs=[rows, head_spec(0), head_spec(0), grads, grads],
        out_shape=[
            sds((seqs * MAXM, D), BF),
            sds((t, D), BF),
            sds((t, D), BF),
            sds((seqs, 2 * RANK, D), F32),
            sds((seqs, 2 * RANK, D), F32),
        ],
        compiler_params=params(2),
        name="attn_bwd_rows",
    )(qkv, qkv, qkv, g, pos, u)


def dh_pick_kernel(dr1_ref, dq_ref, dk_ref, dv_ref, pos_ref, w_ref, o_ref):
    rows = dr1_ref[...] + nt(dq_ref[...], w_ref[:, 0:D])
    high = rows.astype(BF)
    rest = (rows - high.astype(F32)).astype(BF)
    onehot = (lax.broadcasted_iota(jnp.int32, (LEN, MAXM), 0) == pos_ref[0]).astype(BF)
    o_ref[...] = (
        nt(dk_ref[...], w_ref[:, D : 2 * D])
        + nt(dv_ref[...], w_ref[:, 2 * D : 3 * D])
        + nn(onehot, high)
        + nn(onehot, rest)
    )


def dh_pick_call(dr1, dq, dk, dv, pos_row, wp):
    t = dk.shape[0]
    rows = pl.BlockSpec((MAXM, D), lambda s: (s, 0))
    block = pl.BlockSpec((LEN, D), lambda s: (s, 0))
    return pl.pallas_call(
        dh_pick_kernel,
        grid=(t // LEN,),
        in_specs=[rows, rows, block, block, pl.BlockSpec((1, 1, MAXM), lambda s: (s, 0, 0)), whole((D, 3 * D))],
        out_specs=block,
        out_shape=sds((t, D), F32),
        compiler_params=params(),
        name="dh_rows",
    )(dr1, dq, dk, dv, pos_row, wp)


def ffn_back_kernel(e_ref, n1_ref, s1_ref, n2_ref, s2_ref, gp_ref, wo_ref, win_ref, wout_ref, par_ref,
                    dr1_ref, dctx_ref, d2_ref, acc_ref):
    j = pl.program_id(0)
    t = e_ref.shape[0]

    @pl.when(j == 0)
    def _():
        for r in range(0, t, ROWS):
            w = slice(r, r + ROWS)
            d2 = norm_back(e_ref[w, :], n2_ref[w, :].astype(F32), s2_ref[w, :], par_ref[6:7, :])
            d2_ref[w, :] = d2.astype(BF)
            acc_ref[w, :] = d2

    win = flat(win_ref)
    wout = flat(wout_ref)
    for r in range(0, t, ROWS):
        w = slice(r, r + ROWS)
        df = (nt(d2_ref[w, :], wout) * gp_ref[w, :].astype(F32)).astype(BF)
        acc_ref[w, :] += nt(df, win)

    @pl.when(j == 3)
    def _():
        wo = flat(wo_ref)
        for r in range(0, t, ROWS):
            w = slice(r, r + ROWS)
            d1 = norm_back(acc_ref[w, :], n1_ref[w, :].astype(F32), s1_ref[w, :], par_ref[3:4, :])
            dr1_ref[w, :] = d1
            dctx_ref[w, :] = nt(d1.astype(BF), wo).astype(BF)


def ffn_back_call(e, n1, s1, n2, s2, gp, weights, par):
    t = e.shape[0]
    return pl.pallas_call(
        ffn_back_kernel,
        grid=(4,),
        in_specs=[
            whole((t, D)),
            whole((t, D)),
            whole((t, 1)),
            whole((t, D)),
            whole((t, 1)),
            pl.BlockSpec((t, D), lambda j: (0, j)),
            unit_spec(weights["o"], lambda j: 0),
            unit_spec(weights["in"], lambda j: j),
            out_spec(weights["out"], lambda j: j),
            whole(par.shape),
        ],
        out_specs=[whole((t, D)), whole((t, D))],
        out_shape=[sds((t, D), F32), sds((t, D), BF)],
        scratch_shapes=[pltpu.VMEM((t, D), BF), pltpu.VMEM((t, D), F32)],
        compiler_params=params(),
        name="ffn_bwd",
    )(e, n1, s1, n2, s2, gp, weights["o"][0], weights["in"][0], weights["out"][0], par)


def attn_back_kernel(q_ref, k_ref, v_ref, g_ref, z_ref, u_ref, dq_ref, dk_ref, dv_ref, gq_ref, gv_ref):
    low = lax.broadcasted_iota(jnp.int32, (LEN, 2 * HD), 1) < HD
    q = q_ref[...]
    qsc = q * jnp.asarray(SCALE, BF)
    k = k_ref[...]
    v = v_ref[...]
    g = g_ref[...]
    zt = z_ref[...].T
    kt = k.T
    dqs, dks, dvs = [], [], []
    for h in range(2):
        mine = low if h == 0 else jnp.logical_not(low)
        st = nt(k, jnp.where(mine, qsc, jnp.zeros_like(q)))
        pt = jnp.exp(st - zt[h * HD : h * HD + 1, :])
        dpt = nt(v, jnp.where(mine, g, jnp.zeros_like(g)))
        ds = (pt * (dpt - jnp.sum(pt * dpt, axis=0, keepdims=True))).astype(BF)
        dvs.append(nn(pt.astype(BF), g))
        dks.append(nn(ds, q))
        dqs.append(nn(kt[h * HD : (h + 1) * HD, :], ds))
    dq = (jnp.concatenate(dqs, axis=0).T * SCALE).astype(BF)
    dv = jnp.where(low, dvs[0], dvs[1]).astype(BF)
    dq_ref[...] = dq
    dk_ref[...] = (jnp.where(low, dks[0], dks[1]) * SCALE).astype(BF)
    dv_ref[...] = dv
    gq_ref[0] = 2.0 * tn(u_ref[...], dq)
    gv_ref[0] = 2.0 * tn(u_ref[...], dv)


def attn_back_call(qkv, g, z, u):
    t = qkv.shape[0]
    seqs = t // LEN
    grads = pl.BlockSpec((1, 2 * RANK, 2 * HD), lambda s, h: (s, 0, h))
    return pl.pallas_call(
        attn_back_kernel,
        grid=(seqs, PAIRS),
        in_specs=[
            head_spec(0),
            head_spec(1),
            head_spec(2),
            head_spec(0),
            head_spec(0),
            pl.BlockSpec((LEN, 2 * RANK), lambda s, h: (s, 0)),
        ],
        out_specs=[head_spec(0), head_spec(0), head_spec(0), grads, grads],
        out_shape=[sds((t, D), BF)] * 3 + [sds((seqs, 2 * RANK, D), F32)] * 2,
        compiler_params=params(2),
        name="attn_bwd",
    )(qkv, qkv, qkv, g, z, u)


def dh_kernel(dr1_ref, dq_ref, dk_ref, dv_ref, w_ref, o_ref):
    o_ref[...] = (
        dr1_ref[...]
        + nt(dq_ref[...], w_ref[:, 0:D])
        + nt(dk_ref[...], w_ref[:, D : 2 * D])
        + nt(dv_ref[...], w_ref[:, 2 * D : 3 * D])
    )


def dh_call(dr1, dq, dk, dv, wp):
    t = dk.shape[0]
    block = pl.BlockSpec((ROWS, D), lambda i: (i, 0))
    return pl.pallas_call(
        dh_kernel,
        grid=(t // ROWS,),
        in_specs=[block, block, block, block, whole((D, 3 * D))],
        out_specs=block,
        out_shape=sds((t, D), F32),
        compiler_params=params(),
        name="dh",
    )(dr1, dq, dk, dv, wp)


def network(tokens, cotangent, positions, counts, weights, smalls, biases, query_up, value_up):
    seqs = tokens.shape[0]
    x = tokens.reshape(seqs * LEN, D)
    pos_col = positions.reshape(seqs * MAXM, 1)
    pos_row = positions.reshape(seqs, 1, MAXM)
    cot = cotangent.reshape(seqs * MAXM, D)
    h = x
    saved = []
    for layer in range(LAYERS):
        small = smalls[layer]
        par = small.astype(F32).T
        down = small[:, 8 : 8 + 2 * RANK]
        zero = jnp.zeros((RANK, D), BF)
        up3 = jnp.stack(
            [
                jnp.concatenate([2.0 * query_up[layer].astype(BF), zero]),
                jnp.concatenate([zero, zero]),
                jnp.concatenate([zero, 2.0 * value_up[layer].astype(BF)]),
            ]
        )
        bias3 = jnp.stack([par[0:1], jnp.zeros((1, D), F32), par[1:2]])
        keep = layer < LAYERS - 1
        qkv, u, wp = qkv_call(x, weights[layer], down, up3, bias3)
        ctx, z = attn_call(qkv)
        outs = ffn_call(h, ctx, weights[layer], par, biases[layer], keep)
        x, n1, s1, n2, s2 = outs[:5]
        gp = None
        if keep:
            h, gp = outs[5:]
        saved.append((qkv, u, wp, z, n1, s1, n2, s2, gp, par))
    activations = x.reshape(tokens.shape)

    grads = [None] * LAYERS
    qkv, u, wp, z, n1, s1, n2, s2, gp, par = saved[-1]
    dr1, dctx = ffn_pick_call(
        cot, pos_col, counts, n1, s1, n2, s2, weights[-1], par, biases[-1]
    )
    dq, dk, dv, gq, gv = attn_pick_call(qkv, dctx, pos_col, u)
    grads[-1] = (gq, gv)
    e = dh_pick_call(dr1, dq, dk, dv, pos_row, wp)
    for layer in reversed(range(LAYERS - 1)):
        qkv, u, wp, z, n1, s1, n2, s2, gp, par = saved[layer]
        dr1, dctx = ffn_back_call(e, n1, s1, n2, s2, gp, weights[layer], par)
        dq, dk, dv, gq, gv = attn_back_call(qkv, dctx, z, u)
        grads[layer] = (gq, gv)
        e = dh_call(dr1, dq, dk, dv, wp)
    out = []
    for gq, gv in grads:
        out.append(
            jnp.concatenate([jnp.sum(gq, 0)[:RANK], jnp.sum(gv, 0)[RANK:]])
        )
    return activations, e.reshape(tokens.shape), out


ORDERS = ((8, 2, 16, 4), (16, 4, 8, 2))
STEPS = 4
HALF = D // 2


def swap_cores(v, n):
    return lax.ppermute(v, AXES, [(d, d ^ 1) for d in range(n)])


def double_step(v, n, step):
    return lax.ppermute(v, AXES, [(d, d ^ ORDERS[d & 1][step]) for d in range(n)])


def gather_pieces(pair, n):
    held = pair
    for step in range(STEPS - 1):
        held = jnp.concatenate([held, double_step(held, n, step)])
    last = double_step(held, n, STEPS - 1)
    return held, last, swap_cores(held, n), swap_cores(last, n)


def piece_table(me):
    slot = jnp.arange(16, dtype=jnp.int32)

    def order(core, i):
        return jnp.where(core == 0, ORDERS[0][i], ORDERS[1][i])

    def held(device):
        core = device & 1
        rel = slot & 1
        for i in range(STEPS - 1):
            rel = rel + ((slot >> (i + 1)) & 1) * order(core, i)
        first = device ^ rel
        return [first, first ^ order(core, STEPS - 1)]

    return jnp.stack(held(me) + held(me ^ 1))


def arrange_kernel(table_ref, core_ref, a_ref, b_ref, c_ref, d_ref, o_ref, sem):
    own = pl.multiple_of(core_ref[0] * HALF, HALF)
    other = pl.multiple_of(HALF - own, HALF)

    def body(i, carry):
        for k, (ref, lane) in enumerate(((a_ref, own), (b_ref, own), (c_ref, other), (d_ref, other))):
            pltpu.make_async_copy(
                ref.at[i], o_ref.at[table_ref[k, i], :, pl.ds(lane, HALF)], sem
            ).start()
        return carry

    lax.fori_loop(0, 16, body, 0)
    pltpu.make_async_copy(o_ref, o_ref, sem).wait()


def arrange_call(table, core, pieces):
    rows = pieces[0].shape[1]
    anywhere = pl.BlockSpec(memory_space=pl.ANY)
    smem = pl.BlockSpec(memory_space=pltpu.SMEM)
    return pl.pallas_call(
        arrange_kernel,
        in_specs=[smem, smem] + [anywhere] * 4,
        out_specs=anywhere,
        out_shape=sds((32, rows, D), BF),
        scratch_shapes=[pltpu.SemaphoreType.DMA],
        name="arrange",
    )(table, core, *pieces)


def column_blocks(w, n):
    return [w[:, i * D : (i + 1) * D] for i in range(n)]


def plain_gather(w_qkv, w_o, w_in, b_in, w_out, small):
    def gather(v, axis):
        return lax.all_gather(v, AXES, axis=axis, tiled=True)

    weights, smalls, biases = [], [], []
    for layer in range(LAYERS):
        units = column_blocks(gather(w_qkv[layer], 0), 3) + [gather(w_o[layer], 0)]
        units += column_blocks(gather(w_in[layer], 0), 4) + [gather(w_out[layer], 0)]
        packed = jnp.concatenate(units)[None]
        weights.append({"qkv": (packed, 0), "o": (packed, 3), "in": (packed, 4), "out": (packed, 2)})
        smalls.append(gather(small[layer], 0))
        biases.append(gather(b_in[layer], 0).reshape(1, FF).astype(F32))
    return weights, smalls, biases


def fast_gather(n, w_qkv, w_o, w_in, b_in, w_out, small):
    me = lax.axis_index(AXES).astype(jnp.int32)
    core = me & 1
    rb = D // n
    second = lax.all_gather(
        jnp.concatenate([w_out[1], w_o[1]] + column_blocks(w_in[1], 4)), AXES, axis=0, tiled=False
    )
    tiny = jnp.concatenate([small.transpose(1, 0, 2).reshape(rb, -1), b_in.reshape(LAYERS, rb, 4).transpose(1, 0, 2).reshape(rb, -1)], axis=1)
    tiny = jnp.pad(tiny, ((0, 0), (0, 128 - tiny.shape[1]))).reshape(-1, D)
    tiny = jnp.pad(tiny, ((0, 8 - tiny.shape[0]), (0, 0)))
    chunks = [
        column_blocks(w_qkv[0], 3) + [tiny],
        [w_o[0]] + column_blocks(w_in[0], 4),
        [w_out[0]],
        column_blocks(w_qkv[1], 3),
    ]
    sizes = [sum(v.shape[0] for v in c) for c in chunks]
    rows = jnp.concatenate([v for c in chunks for v in c])
    first_half, second_half = rows[:, :HALF], rows[:, HALF:]
    keep = jnp.where(core == 0, first_half, second_half)
    give = jnp.where(core == 0, second_half, first_half)
    pairs = jnp.stack([keep, swap_cores(give, n)])
    table = piece_table(me)
    packed = []
    at = 0
    for size in sizes:
        packed.append(arrange_call(table, core[None], gather_pieces(pairs[:, at : at + size], n)))
        at += size
    weights = [
        {"qkv": (packed[0], 0), "o": (packed[1], 0), "in": (packed[1], 1), "out": (packed[2], 0)},
        {"qkv": (packed[3], 0), "o": (second, 4), "in": (second, 5), "out": (second, 0)},
    ]
    tiny = packed[0][:, 3 * rb : 3 * rb + rb * 128 // D].reshape(D, 128)
    width = small.shape[2]
    smalls = [tiny[:, i * width : (i + 1) * width] for i in range(LAYERS)]
    at = LAYERS * width
    biases = [tiny[:, at + 4 * i : at + 4 * i + 4].reshape(1, FF).astype(F32) for i in range(LAYERS)]
    return weights, smalls, biases


def total(v, n):
    if n & (n - 1):
        return lax.psum(v, AXES)
    step = 1
    while step < n:
        v = v + lax.ppermute(v, AXES, [(d, d ^ step) for d in range(n)])
        step *= 2
    return v


def on_device(
    sizes, tokens, cotangent, positions, counts, w_qkv, w_o, w_in, b_in, w_out, small, query_up, value_up
):
    n = sizes[0] * sizes[1]
    frozen = (w_qkv, w_o, w_in, b_in, w_out, small)
    if sizes == (16, 2):
        weights, smalls, biases = fast_gather(n, *frozen)
    else:
        weights, smalls, biases = plain_gather(*frozen)
    activations, d_tokens, grads = network(
        tokens, cotangent, positions, counts, weights, smalls, biases, query_up, value_up
    )
    g = total(jnp.stack(grads), n)
    return activations, d_tokens, g[:, :RANK], g[:, RANK:]


def solution(mesh):
    both = P(AXES, None, None)
    mid = P(None, AXES, None)
    in_specs = (both, both, P(AXES, None), P(AXES), mid, mid, mid, P(None, AXES), mid, mid, P(), P())
    out_specs = (both, both, P(), P())
    sizes = (mesh.shape["dp"], mesh.shape["fsdp"])
    return jax.shard_map(
        functools.partial(on_device, sizes), mesh=mesh, in_specs=in_specs, out_specs=out_specs, check_vma=False
    )
```
